32 devices in a mesh: groups: 2 (over x), module: 16 (over z, y, core).
Axes of the slice: x: 2, y: 2, z: 4, core: 2. Of those that a mesh axis runs over, the one named last changes fastest.
Arguments:
- act_table: bfloat16 [4096, 1024], P(('groups', 'module')), parts along dimension 0, may hold values from -6 to 6
- grad_table: bfloat16 [4096, 1024], P(('groups', 'module')), parts along dimension 0, may hold values from -6 to 6
- token_rows: int32 [256, 128], P(('groups', 'module')), parts along dimension 0, may hold values from 0 to 127
- left_inv: bfloat16 [16, 64, 64], P('module'), may hold values from -3 to 3.5
- right_inv: bfloat16 [16, 64, 64], P('module'), may hold values from -3 to 3.5
- query_grads: bfloat16 [256, 16, 4096], P('groups', 'module'), parts along dimension 0, may hold values from -0.03125 to 0.03125
Outputs:
- scores: float32 [256, 128], P(('groups', 'module')), parts along dimension 0
The draws below stay inside these ranges and needn't reach their ends.
There are 2 independent parts, one for each index of `groups`. The reference program is written for one: setup_inputs(seed, part) draws one part's arguments, and reference() takes and returns one part's arrays. A program takes and returns all parts, laid end to end along the dimension named above; an argument that names none is the same for every part. Nothing has to cross between parts.
Inputs may be any that keep to these rules, and one draw needn't show every extreme that they name: `token_rows`: each example's rows index the 128 table rows held with its block of 8 examples (the block's token states are stored deduplicated, so tokens of the block share these rows).
All inputs are finite; a program needn't handle non-finite values.
Results may differ from the reference program's by a relative error of at most 0.0049.
Values may be sent and summed in bfloat16 or wider, within the bound.
No kernel may reach another device: no remote copies, remote signals or barrier semaphores. Data moves between devices by JAX's collectives and lax.ppermute only.
A program may use at most 128 MiB of HBM per device.

```python
import math
import jax
import jax.numpy as jnp
from jax import lax

R = 64
TOKS = 128
E_DEV = 8
TAB_DEV = 128
M = 16
EX = 128
NQ = 128
ROWS = 2048


def factor_draw(key):
    base = jax.random.uniform(key, (M, R, R), jnp.float32, -1.7, 1.7)
    return jnp.einsum('mij,mkj->mik', base, base) / R + 0.5 * jnp.eye(R, dtype=jnp.float32)


def draw_left_inv(key, part):
    return factor_draw(jax.random.fold_in(key, 11)).astype(jnp.bfloat16)


def draw_right_inv(key, part):
    return factor_draw(jax.random.fold_in(key, 12)).astype(jnp.bfloat16)


def place_ends(array, own_key, smallest, top_value):
    shape = array.shape
    index_at = [jax.random.randint(jax.random.fold_in(own_key, axis), (), 0, shape[axis]) for axis in range(len(shape))]
    array = array.at[tuple(index_at)].set(smallest)
    longest = shape.index(max(shape))
    index_at[longest] = (index_at[longest] + 1) % shape[longest]
    return array.at[tuple(index_at)].set(top_value)


def strengthened(entries, own_key, source, target, blocks, factor):
    owner, partner = [(jnp.arange(entries.shape[axis_at]) // (entries.shape[axis_at] // blocks)).reshape([-1 if axis == axis_at else 1 for axis in range(entries.ndim)]) for axis_at in (source, target)]
    chosen = jax.random.permutation(own_key, blocks)[partner]
    strong = (owner == chosen) | (owner == (partner + blocks // 2) % blocks)
    return jnp.where(strong, factor * entries, entries)


def block_scale(stream_key, dims, split, low, high):
    factor_of, own = 1.0, jax.random.fold_in(stream_key, 6)
    for dim, parts in split:
        heights = jnp.exp(jax.random.uniform(jax.random.fold_in(own, dim), (parts,), jnp.float32, low / len(split), high / len(split)))
        factor_of = factor_of * jnp.repeat(heights, dims[dim] // parts).reshape([-1 if axis == dim else 1 for axis in range(len(dims))])
    return factor_of


def centred(key, extent, spread, bound, cuts=(), kind=jnp.bfloat16):
    values = jax.random.normal(key, extent, jnp.float32) * spread
    if len(cuts) > 0:
        values = block_scale(key, extent, cuts, -0.22, 0.18) * values
    return jnp.clip(values, min=-bound, max=bound).astype(kind)


def gaussian_with(own_key, shape, spread, reach, split, heavy, kind=jnp.bfloat16):
    entries = spread * jax.random.normal(own_key, shape, jnp.float32)
    if split:
        entries = entries * block_scale(own_key, shape, split, -0.22, 0.18)
    return jnp.clip(strengthened(entries, jax.random.fold_in(own_key, 3), *heavy), -reach, reach).astype(kind)


def setup_inputs(seed: int = 0, part: int = 0) -> dict:
    splits = jax.random.split(jax.random.key(seed), 7)
    part_keys = jax.random.split(jax.random.fold_in(splits[6], part), 7)
    return {
        "act_table": centred(part_keys[0], (ROWS, M * R), 1.0, 6.0, ((0, 16),)),
        "grad_table": centred(part_keys[1], (ROWS, M * R), 1.0, 6.0, ((0, 16),)),
        "token_rows": place_ends(jax.random.randint(part_keys[2], (EX, TOKS), 0, TAB_DEV), jax.random.fold_in(part_keys[2], 1), 0, TAB_DEV - 1).astype(jnp.int32),
        "left_inv": draw_left_inv(jax.random.fold_in(splits[6], 71), part),
        "right_inv": draw_right_inv(jax.random.fold_in(splits[6], 71), part),
        "query_grads": gaussian_with(part_keys[5], (NQ, M, R * R), (M * R * R) ** -0.5, 0.03125, ((1, 16),), (1, 0, 16, 2.0)),
    }


def reference(act_table, grad_table, token_rows, left_inv, right_inv, query_grads):
    owner = jnp.arange(EX, dtype=jnp.int32) // E_DEV * TAB_DEV
    table_rows = token_rows + owner[:, None]

    def module_term(total, module_index):
        acts = lax.dynamic_slice_in_dim(act_table, module_index * R, R, 1)[table_rows]
        grads = lax.dynamic_slice_in_dim(grad_table, module_index * R, R, 1)[table_rows]
        outer_sum = jnp.einsum('eti,etj->eij', grads.astype(jnp.float32), acts.astype(jnp.float32)) / math.sqrt(TOKS)
        per_example = lax.optimization_barrier(outer_sum.astype(jnp.bfloat16))
        middle_sum = jnp.einsum('ejk,kl->ejl', per_example.astype(jnp.float32), right_inv[module_index].astype(jnp.float32))
        middle = lax.optimization_barrier(middle_sum.astype(jnp.bfloat16))
        conditioned = jnp.einsum('ij,ejl->eil', left_inv[module_index].astype(jnp.float32), middle.astype(jnp.float32)).astype(jnp.bfloat16)
        queries = query_grads[:, module_index, :]
        term = jnp.dot(queries, conditioned.reshape(EX, R * R).T, preferred_element_type=jnp.float32)
        return (total + term, None)
    total, _ = lax.scan(module_term, jnp.zeros((NQ, EX), jnp.float32), jnp.arange(M, dtype=jnp.int32))
    return total
```

```python
import functools
import math

import jax
import jax.numpy as jnp
from jax import lax
from jax.experimental import pallas as pl
from jax.experimental.pallas import tpu as pltpu
from jax.sharding import PartitionSpec as P


def pack_kernel(act_ref, grad_ref, tok_ref, out_ref):
    owners = out_ref.shape[0]
    rows = act_ref.shape[0]
    rank = act_ref.shape[1] // owners
    examples, tokens = tok_ref.shape
    for owner in range(owners):
        columns = slice(owner * rank, (owner + 1) * rank)
        out_ref[owner, :rows, :] = jnp.concatenate([grad_ref[:, columns], act_ref[:, columns]], axis=1)
    tok = tok_ref[...]
    row_of_lane = lax.broadcasted_iota(jnp.int32, (examples, rows), 1)
    counts = jnp.zeros((examples, rows), jnp.float32)
    for t in range(tokens):
        counts += jnp.where(tok[:, t : t + 1] == row_of_lane, 1.0, 0.0)
    counts = counts.astype(jnp.bfloat16)
    for owner in range(owners):
        out_ref[owner, rows:, :] = counts


def owner_kernel(scale, recv_hbm, query_hbm, left_ref, right_ref, out_ref, recv, query, spread, grads, cond, recv_sem, query_sem):
    blocks, height, width = recv.shape
    rank = left_ref.shape[-1]
    rows = width
    examples = height - rows
    half = rank // 2
    arrivals = [pltpu.make_async_copy(recv_hbm.at[b], recv.at[b], recv_sem.at[b]) for b in range(blocks)]
    for copy in arrivals:
        copy.start()
    query_copy = pltpu.make_async_copy(query_hbm, query, query_sem)
    query_copy.start()

    left = left_ref[0]
    right = right_ref[0]
    spread[...] = jnp.zeros_like(spread)
    spread[rank:, :rank] = right
    spread[rank:, 3 * rank :] = right

    def one(b):
        table = recv[b, :rows, :]
        counts = recv[b, rows:, :].astype(jnp.float32)
        slot = b % grads.shape[0]
        grads[slot] = lax.dot_general(left, table[:, :rank], (((1,), (1,)), ((), ())), preferred_element_type=jnp.float32)
        acts = jnp.dot(table, spread[...], preferred_element_type=jnp.float32)
        high = acts.astype(jnp.bfloat16)
        low = (acts - high.astype(jnp.float32)).astype(jnp.bfloat16)
        weights = jnp.concatenate(
            [
                jnp.concatenate([high[:, :width], low[:, :width]], axis=1),
                jnp.concatenate([high[:, width:], low[:, width:]], axis=1),
            ],
            axis=0,
        )
        columns = []
        for parity in range(2):
            pieces = [grads[slot, pl.ds(2 * p + parity, 1), :] * counts for p in range(half)]
            columns.append(jnp.concatenate(pieces, axis=0).astype(jnp.bfloat16))
        weighted = jnp.concatenate(columns, axis=1)
        product = jnp.dot(weighted, weights, preferred_element_type=jnp.float32)
        return product[:, :width] + product[:, width:]

    for b in range(0, blocks, 2):
        arrivals[b].wait()
        arrivals[b + 1].wait()
        first, second = one(b), one(b + 1)
        for p in range(half):
            piece = slice(p * examples, (p + 1) * examples)
            cond[b * examples : (b + 2) * examples, p * width : (p + 1) * width] = jnp.concatenate(
                [first[piece], second[piece]], axis=0
            ).astype(jnp.bfloat16)

    query_copy.wait()
    scores = lax.dot_general(query[...], cond[...], (((1,), (1,)), ((), ())), preferred_element_type=jnp.float32)
    out_ref[...] = scores * scale


def per_device(owners, act_table, grad_table, token_rows, left_inv, right_inv, query_grads):
    rows, columns = act_table.shape
    examples, tokens = token_rows.shape
    local_modules, rank, _ = left_inv.shape
    queries = query_grads.shape[0]
    width = 2 * rank
    assert local_modules == 1 and columns == owners * rank
    assert rows == width and tokens <= 256 and examples % 8 == 0
    height = rows + examples

    packed = pl.pallas_call(
        pack_kernel,
        out_shape=jax.ShapeDtypeStruct((owners, height, width), jnp.bfloat16),
        name="pack",
    )(act_table, grad_table, token_rows)
    recv = lax.all_to_all(packed, "module", split_axis=0, concat_axis=0, tiled=True)

    partial = pl.pallas_call(
        functools.partial(owner_kernel, 1.0 / math.sqrt(tokens)),
        out_shape=jax.ShapeDtypeStruct((queries, owners * examples), jnp.float32),
        in_specs=[
            pl.BlockSpec(memory_space=pl.ANY),
            pl.BlockSpec(memory_space=pl.ANY),
            pl.BlockSpec(memory_space=pltpu.VMEM),
            pl.BlockSpec(memory_space=pltpu.VMEM),
        ],
        out_specs=pl.BlockSpec(memory_space=pltpu.VMEM),
        scratch_shapes=[
            pltpu.VMEM((owners, height, width), jnp.bfloat16),
            pltpu.VMEM((queries, rank * rank), jnp.bfloat16),
            pltpu.VMEM((width, 2 * width), jnp.bfloat16),
            pltpu.VMEM((4, rank, rows), jnp.float32),
            pltpu.VMEM((owners * examples, rank * rank), jnp.bfloat16),
            pltpu.SemaphoreType.DMA((owners,)),
            pltpu.SemaphoreType.DMA,
        ],
        name="owner",
    )(recv, query_grads.reshape(queries, rank * rank), left_inv, right_inv)

    tiles = partial.reshape(owners, queries // owners, owners * examples)
    gathered = lax.all_to_all(tiles, "module", split_axis=0, concat_axis=0, tiled=True)
    return jnp.sum(gathered, axis=0)


def solution(mesh):
    placed = (
        P(("groups", "module"), None),
        P(("groups", "module"), None),
        P(("groups", "module"), None),
        P("module", None, None),
        P("module", None, None),
        P("groups", "module", None),
    )
    return jax.shard_map(
        functools.partial(per_device, mesh.shape["module"]),
        mesh=mesh,
        in_specs=placed,
        out_specs=P(("groups", "module"), None),
        check_vma=False,
    )
```

```python
import functools
import math

import jax
import jax.numpy as jnp
from jax import lax
from jax.experimental import pallas as pl
from jax.experimental.pallas import tpu as pltpu
from jax.sharding import PartitionSpec as P

VMEM_LIMIT = 32 * 1024 * 1024


def pack_kernel(act_ref, grad_ref, tok_ref, out_ref):
    owners = out_ref.shape[0]
    rows = act_ref.shape[0]
    rank = act_ref.shape[1] // owners
    half = rows // 2
    examples, tokens = tok_ref.shape
    for owner in range(0, owners, 2):
        pair = slice(owner * rank, (owner + 2) * rank)
        turned = grad_ref[:, pair].T
        acts = act_ref[:, pair]
        for side in range(2):
            columns = slice(side * rank, (side + 1) * rank)
            out_ref[owner + side, :rank, :] = turned[columns, :]
            out_ref[owner + side, rank : rank + half, :] = jnp.concatenate(
                [acts[:half, columns], acts[half:, columns]], axis=1
            )
    tok = tok_ref[...]
    row_of_lane = lax.broadcasted_iota(jnp.int32, (examples, rows), 1)
    counts = jnp.zeros((examples, rows), jnp.float32)
    for t in range(tokens):
        counts += jnp.where(tok[:, t : t + 1] == row_of_lane, 1.0, 0.0)
    counts = counts.astype(jnp.bfloat16)
    for owner in range(owners):
        out_ref[owner, rank + half :, :] = counts


def query_kernel(query_ref, left_ref, right_ref, out_ref, diagonal, turned):
    rank = left_ref.shape[-1]
    tiles, _, lanes = turned.shape
    step = diagonal.shape[0]
    right = right_ref[0]
    diagonal[...] = jnp.zeros_like(diagonal)
    for at in range(0, step, rank):
        diagonal[at : at + rank, at : at + rank] = right
    left = left_ref[0].astype(jnp.float32).T.astype(jnp.bfloat16)
    left = jnp.concatenate([left, left], axis=1)
    for tile in range(tiles):
        columns = slice(tile * lanes, (tile + 1) * lanes)
        for at in range(0, rank * rank, step):
            turned[tile, at : at + step, :] = lax.dot_general(
                diagonal[...],
                query_ref[columns, at : at + step],
                (((1,), (1,)), ((), ())),
                preferred_element_type=jnp.float32,
            )
        for k in range(0, rank, 2):
            value = jnp.concatenate([turned[tile, pl.ds(k + s, rank, stride=rank), :] for s in range(2)], axis=1)
            high = value.astype(jnp.bfloat16)
            low = (value - high.astype(jnp.float32)).astype(jnp.bfloat16)
            product = jnp.dot(left, jnp.concatenate([high, low], axis=0), preferred_element_type=jnp.float32)
            for s in range(2):
                turned[tile, pl.ds(k + s, rank, stride=rank), :] = product[:, s * lanes : (s + 1) * lanes]
        out_ref[:, columns] = turned[tile].astype(jnp.bfloat16)


def owner_kernel(scale, recv, query, out_ref, grads, per_example):
    blocks, height, width = recv.shape
    rank = grads.shape[1]
    rows = width
    half_rows = rows // 2
    examples = height - rank - half_rows
    pairs = rank // 2
    first_half = lax.broadcasted_iota(jnp.int32, (half_rows, width), 1) < rank

    def one(b):
        counts = recv[b, rank + half_rows :, :].astype(jnp.float32)
        slot = b % grads.shape[0]
        grads[slot] = recv[b, :rank, :].astype(jnp.float32)
        acts = recv[b, rank : rank + half_rows, :]
        swapped = jnp.concatenate([acts[:, rank:], acts[:, :rank]], axis=1)
        zero = jnp.zeros_like(acts)
        weights = jnp.concatenate(
            [
                jnp.where(first_half, acts, zero),
                jnp.where(first_half, swapped, zero),
                jnp.where(first_half, zero, swapped),
                jnp.where(first_half, zero, acts),
            ],
            axis=0,
        )
        columns = []
        for parity in range(2):
            pieces = [grads[slot, pl.ds(2 * p + parity, 1), :] * counts for p in range(pairs)]
            columns.append(jnp.concatenate(pieces, axis=0).astype(jnp.bfloat16))
        weighted = jnp.concatenate(columns, axis=1)
        return jnp.dot(weighted, weights, preferred_element_type=jnp.float32) * scale

    for b in range(0, blocks, 2):
        first, second = one(b), one(b + 1)
        for p in range(pairs):
            piece = slice(p * examples, (p + 1) * examples)
            per_example[b * examples : (b + 2) * examples, p * width : (p + 1) * width] = jnp.concatenate(
                [first[piece], second[piece]], axis=0
            ).astype(jnp.bfloat16)

    out_ref[...] = jnp.dot(per_example[...], query[...], preferred_element_type=jnp.float32).T


def per_device(owners, act_table, grad_table, token_rows, left_inv, right_inv, query_grads):
    rows, columns = act_table.shape
    examples, tokens = token_rows.shape
    local_modules, rank, _ = left_inv.shape
    queries = query_grads.shape[0]
    width = 2 * rank
    lanes = min(queries, 128)
    assert queries % lanes == 0
    assert local_modules == 1 and columns == owners * rank and owners % 2 == 0
    assert rows == width and tokens <= 256 and examples % 8 == 0
    height = rank + rows // 2 + examples

    packed = pl.pallas_call(
        pack_kernel,
        out_shape=jax.ShapeDtypeStruct((owners, height, width), jnp.bfloat16),
        compiler_params=pltpu.CompilerParams(vmem_limit_bytes=VMEM_LIMIT),
        name="pack",
    )(act_table, grad_table, token_rows)
    recv = lax.all_to_all(packed, "module", split_axis=0, concat_axis=0, tiled=True)

    prepared = pl.pallas_call(
        query_kernel,
        out_shape=jax.ShapeDtypeStruct((rank * rank, queries), jnp.bfloat16),
        scratch_shapes=[
            pltpu.VMEM((4 * rank, 4 * rank), jnp.bfloat16),
            pltpu.VMEM((queries // lanes, rank * rank, lanes), jnp.float32),
        ],
        cost_estimate=pl.CostEstimate(
            flops=4 * queries * rank**3, bytes_accessed=4 * queries * rank**2, transcendentals=0
        ),
        compiler_params=pltpu.CompilerParams(vmem_limit_bytes=VMEM_LIMIT),
        name="prepare",
    )(query_grads.reshape(queries, rank * rank), left_inv, right_inv)

    partial = pl.pallas_call(
        functools.partial(owner_kernel, 1.0 / math.sqrt(tokens)),
        out_shape=jax.ShapeDtypeStruct((queries, owners * examples), jnp.float32),
        scratch_shapes=[
            pltpu.VMEM((4, rank, rows), jnp.float32),
            pltpu.VMEM((owners * examples, rank * rank), jnp.bfloat16),
        ],
        compiler_params=pltpu.CompilerParams(vmem_limit_bytes=VMEM_LIMIT),
        name="owner",
    )(recv, prepared)

    tiles = partial.reshape(owners, queries // owners, owners * examples)
    gathered = lax.all_to_all(tiles, "module", split_axis=0, concat_axis=0, tiled=True)
    return jnp.sum(gathered, axis=0)


def solution(mesh):
    placed = (
        P(("groups", "module"), None),
        P(("groups", "module"), None),
        P(("groups", "module"), None),
        P("module", None, None),
        P("module", None, None),
        P("groups", "module", None),
    )
    return jax.shard_map(
        functools.partial(per_device, mesh.shape["module"]),
        mesh=mesh,
        in_specs=placed,
        out_specs=P(("groups", "module"), None),
        check_vma=False,
    )
```

```python
import functools
import math

import jax
import jax.numpy as jnp
from jax import lax
from jax.experimental import pallas as pl
from jax.experimental.pallas import tpu as pltpu
from jax.sharding import PartitionSpec as P

VMEM_LIMIT = 32 * 1024 * 1024
CHUNKS = 2


def member_order(members):
    first = members * 11 // 16

    def hops(i):
        return abs((i >> 2) - (first >> 2)) + (((i ^ first) >> 1) & 1)

    return [first] + sorted((i for i in range(members) if i != first), key=lambda i: (-hops(i), i))


def pack_kernel(slots, act_hbm, grad_hbm, tok_hbm, out_hbm, act, grad, tok, packed, in_sem, out_sem):
    owners = out_hbm.shape[0]
    rows = act.shape[0]
    rank = act.shape[1] // owners
    half = rows // 2
    examples, tokens = tok.shape
    chunks = in_sem.shape[0] // 2
    share = owners // chunks
    arrivals = []
    tok_copy = pltpu.make_async_copy(tok_hbm, tok, in_sem.at[2 * chunks])
    tok_copy.start()
    for c in range(chunks):
        columns = pl.ds(c * share * rank, share * rank)
        pair = [
            pltpu.make_async_copy(grad_hbm.at[:, columns], grad.at[:, columns], in_sem.at[2 * c]),
            pltpu.make_async_copy(act_hbm.at[:, columns], act.at[:, columns], in_sem.at[2 * c + 1]),
        ]
        for copy in pair:
            copy.start()
        arrivals.append(pair)

    tok_copy.wait()
    local = tok[...]
    row_of_lane = lax.broadcasted_iota(jnp.int32, (examples, rows), 1)
    counts = jnp.zeros((examples, rows), jnp.float32)
    for t in range(tokens):
        counts += jnp.where(local[:, t : t + 1] == row_of_lane, 1.0, 0.0)
    counts = counts.astype(jnp.bfloat16)

    departures = []
    for c in range(chunks):
        for copy in arrivals[c]:
            copy.wait()
        for owner in range(c * share, (c + 1) * share, 2):
            pair = slice(owner * rank, (owner + 2) * rank)
            turned = grad[:, pair].T
            acts = act[:, pair]
            for side in range(2):
                columns = slice(side * rank, (side + 1) * rank)
                packed[owner + side, :rank, :] = turned[columns, :]
                packed[owner + side, rank : rank + half, :] = jnp.concatenate(
                    [acts[:half, columns], acts[half:, columns]], axis=1
                )
                packed[owner + side, rank + half :, :] = counts
        for owner in range(c * share, (c + 1) * share):
            copy = pltpu.make_async_copy(packed.at[owner], out_hbm.at[slots[owner]], out_sem.at[owner])
            copy.start()
            departures.append(copy)
    for copy in departures:
        copy.wait()


def query_kernel(query_ref, left_ref, right_ref, out_ref, diagonal, turned):
    rank = left_ref.shape[-1]
    tiles, _, lanes = turned.shape
    step = diagonal.shape[0]
    right = right_ref[0]
    diagonal[...] = jnp.zeros_like(diagonal)
    for at in range(0, step, rank):
        diagonal[at : at + rank, at : at + rank] = right
    left = left_ref[0].astype(jnp.float32).T.astype(jnp.bfloat16)
    left = jnp.concatenate([left, left], axis=1)
    for tile in range(tiles):
        columns = slice(tile * lanes, (tile + 1) * lanes)
        for at in range(0, rank * rank, step):
            turned[tile, at : at + step, :] = lax.dot_general(
                diagonal[...],
                query_ref[columns, at : at + step],
                (((1,), (1,)), ((), ())),
                preferred_element_type=jnp.float32,
            )
        for k in range(0, rank, 2):
            value = jnp.concatenate([turned[tile, pl.ds(k + s, rank, stride=rank), :] for s in range(2)], axis=1)
            high = value.astype(jnp.bfloat16)
            low = (value - high.astype(jnp.float32)).astype(jnp.bfloat16)
            product = jnp.dot(left, jnp.concatenate([high, low], axis=0), preferred_element_type=jnp.float32)
            for s in range(2):
                turned[tile, pl.ds(k + s, rank, stride=rank), :] = product[:, s * lanes : (s + 1) * lanes]
        out_ref[:, columns] = turned[tile].astype(jnp.bfloat16)


def owner_kernel(scale, order, slots, recv, query, out_ref, grads, per_example):
    blocks, height, width = recv.shape
    rank = grads.shape[1]
    rows = width
    half_rows = rows // 2
    examples = height - rank - half_rows
    pairs = rank // 2
    first_half = lax.broadcasted_iota(jnp.int32, (half_rows, width), 1) < rank

    def one(b):
        counts = recv[b, rank + half_rows :, :].astype(jnp.float32)
        slot = b % grads.shape[0]
        grads[slot] = recv[b, :rank, :].astype(jnp.float32)
        acts = recv[b, rank : rank + half_rows, :]
        swapped = jnp.concatenate([acts[:, rank:], acts[:, :rank]], axis=1)
        zero = jnp.zeros_like(acts)
        weights = jnp.concatenate(
            [
                jnp.where(first_half, acts, zero),
                jnp.where(first_half, swapped, zero),
                jnp.where(first_half, zero, swapped),
                jnp.where(first_half, zero, acts),
            ],
            axis=0,
        )
        columns = []
        for parity in range(2):
            pieces = [grads[slot, pl.ds(2 * p + parity, 1), :] * counts for p in range(pairs)]
            columns.append(jnp.concatenate(pieces, axis=0).astype(jnp.bfloat16))
        weighted = jnp.concatenate(columns, axis=1)
        return jnp.dot(weighted, weights, preferred_element_type=jnp.float32) * scale

    for b in range(0, blocks, 2):
        first, second = one(slots[b]), one(slots[b + 1])
        for p in range(pairs):
            piece = slice(p * examples, (p + 1) * examples)
            per_example[b * examples : (b + 2) * examples, p * width : (p + 1) * width] = jnp.concatenate(
                [first[piece], second[piece]], axis=0
            ).astype(jnp.bfloat16)

    scores = jnp.dot(per_example[...], query[...], preferred_element_type=jnp.float32).T
    tile = out_ref.shape[1]
    for slot, member in enumerate(order):
        out_ref[slot] = scores[member * tile : (member + 1) * tile]


def per_device(owners, act_table, grad_table, token_rows, left_inv, right_inv, query_grads):
    rows, columns = act_table.shape
    examples, tokens = token_rows.shape
    local_modules, rank, _ = left_inv.shape
    queries = query_grads.shape[0]
    width = 2 * rank
    lanes = min(queries, 128)
    assert queries % lanes == 0
    assert local_modules == 1 and columns == owners * rank and owners % 2 == 0
    assert rows == width and tokens <= 256 and examples % 8 == 0
    height = rank + rows // 2 + examples
    chunks = math.gcd(CHUNKS, owners // 2)

    order = member_order(owners)
    slots = [order.index(member) for member in range(owners)]

    def exchange(pieces):
        return lax.all_to_all(
            pieces, "module", split_axis=0, concat_axis=0, axis_index_groups=[order], tiled=True
        )

    packed = pl.pallas_call(
        functools.partial(pack_kernel, slots),
        out_shape=jax.ShapeDtypeStruct((owners, height, width), jnp.bfloat16),
        in_specs=[pl.BlockSpec(memory_space=pltpu.HBM)] * 3,
        out_specs=pl.BlockSpec(memory_space=pltpu.HBM),
        scratch_shapes=[
            pltpu.VMEM((rows, columns), jnp.bfloat16),
            pltpu.VMEM((rows, columns), jnp.bfloat16),
            pltpu.VMEM((examples, tokens), jnp.int32),
            pltpu.VMEM((owners, height, width), jnp.bfloat16),
            pltpu.SemaphoreType.DMA((2 * chunks + 1,)),
            pltpu.SemaphoreType.DMA((owners,)),
        ],
        name="pack",
    )(act_table, grad_table, token_rows)
    recv = exchange(packed)

    prepared = pl.pallas_call(
        query_kernel,
        out_shape=jax.ShapeDtypeStruct((rank * rank, queries), jnp.bfloat16),
        scratch_shapes=[
            pltpu.VMEM((4 * rank, 4 * rank), jnp.bfloat16),
            pltpu.VMEM((queries // lanes, rank * rank, lanes), jnp.float32),
        ],
        cost_estimate=pl.CostEstimate(
            flops=4 * queries * rank**3, bytes_accessed=4 * queries * rank**2, transcendentals=0
        ),
        compiler_params=pltpu.CompilerParams(vmem_limit_bytes=VMEM_LIMIT),
        name="prepare",
    )(query_grads.reshape(queries, rank * rank), left_inv, right_inv)

    partial = pl.pallas_call(
        functools.partial(owner_kernel, 1.0 / math.sqrt(tokens), order, slots),
        out_shape=jax.ShapeDtypeStruct((owners, queries // owners, owners * examples), jnp.float32),
        scratch_shapes=[
            pltpu.VMEM((4, rank, rows), jnp.float32),
            pltpu.VMEM((owners * examples, rank * rank), jnp.bfloat16),
        ],
        compiler_params=pltpu.CompilerParams(vmem_limit_bytes=VMEM_LIMIT),
        name="owner",
    )(recv, prepared)

    return jnp.sum(exchange(partial), axis=0)


def solution(mesh):
    placed = (
        P(("groups", "module"), None),
        P(("groups", "module"), None),
        P(("groups", "module"), None),
        P("module", None, None),
        P("module", None, None),
        P("groups", "module", None),
    )
    return jax.shard_map(
        functools.partial(per_device, mesh.shape["module"]),
        mesh=mesh,
        in_specs=placed,
        out_specs=P(("groups", "module"), None),
        check_vma=False,
    )
```

```python
import functools
import math

import jax
import jax.numpy as jnp
from jax import lax
from jax.experimental import pallas as pl
from jax.experimental.pallas import tpu as pltpu
from jax.sharding import PartitionSpec as P

VMEM_LIMIT = 32 * 1024 * 1024
FIRST_OUT, FIRST_BACK = 9, 11


def member_order(members, first):
    def hops(i):
        return abs((i >> 2) - (first >> 2)) + (((i ^ first) >> 1) & 1)

    return [first] + sorted((i for i in range(members) if i != first), key=lambda i: (-hops(i), i))


def pack_kernel(slots, act_hbm, grad_hbm, tok_hbm, out_hbm, act, grad, tok, packed, in_sem, out_sem):
    owners = out_hbm.shape[0]
    rows = act.shape[0]
    rank = act.shape[1] // owners
    half = rows // 2
    examples, tokens = tok.shape
    tok_copy = pltpu.make_async_copy(tok_hbm, tok, in_sem.at[0])
    grad_copy = pltpu.make_async_copy(grad_hbm, grad, in_sem.at[1])
    act_copy = pltpu.make_async_copy(act_hbm, act, in_sem.at[2])
    tok_copy.start()
    grad_copy.start()
    act_copy.start()

    tok_copy.wait()
    local = tok[...]
    row_of_lane = lax.broadcasted_iota(jnp.int32, (examples, rows), 1)
    counts = jnp.zeros((examples, rows), jnp.float32)
    for t in range(tokens):
        counts += jnp.where(local[:, t : t + 1] == row_of_lane, 1.0, 0.0)
    counts = counts.astype(jnp.bfloat16)

    grad_copy.wait()
    act_copy.wait()
    departures = []
    ready = set()
    share = owners // out_sem.shape[0]
    for slot in range(owners):
        pair = slots.index(slot) // 2
        if pair not in ready:
            ready.add(pair)
            wide = slice(2 * pair * rank, 2 * (pair + 1) * rank)
            turned = grad[:, wide].T
            acts = act[:, wide]
            for side in range(2):
                columns = slice(side * rank, (side + 1) * rank)
                to = slots[2 * pair + side]
                packed[to, :rank, :] = turned[columns, :]
                packed[to, rank : rank + half, :] = jnp.concatenate([acts[:half, columns], acts[half:, columns]], axis=1)
                packed[to, rank + half :, :] = counts
        if (slot + 1) % share == 0:
            block = pl.ds(slot + 1 - share, share)
            departures.append(pltpu.make_async_copy(packed.at[block], out_hbm.at[block], out_sem.at[slot // share]))
            departures[-1].start()
    for copy in departures:
        copy.wait()


def query_kernel(query_ref, left_ref, right_ref, out_ref, diagonal, turned):
    rank = left_ref.shape[-1]
    tiles, _, lanes = turned.shape
    step = diagonal.shape[0]
    right = right_ref[0]
    diagonal[...] = jnp.zeros_like(diagonal)
    for at in range(0, step, rank):
        diagonal[at : at + rank, at : at + rank] = right
    left = left_ref[0].astype(jnp.float32).T.astype(jnp.bfloat16)
    left = jnp.concatenate([left, left], axis=1)
    for tile in range(tiles):
        columns = slice(tile * lanes, (tile + 1) * lanes)
        for at in range(0, rank * rank, step):
            turned[tile, at : at + step, :] = lax.dot_general(
                diagonal[...],
                query_ref[columns, at : at + step],
                (((1,), (1,)), ((), ())),
                preferred_element_type=jnp.float32,
            )
        for k in range(0, rank, 2):
            value = jnp.concatenate([turned[tile, pl.ds(k + s, rank, stride=rank), :] for s in range(2)], axis=1)
            high = value.astype(jnp.bfloat16)
            low = (value - high.astype(jnp.float32)).astype(jnp.bfloat16)
            product = jnp.dot(left, jnp.concatenate([high, low], axis=0), preferred_element_type=jnp.float32)
            for s in range(2):
                turned[tile, pl.ds(k + s, rank, stride=rank), :] = product[:, s * lanes : (s + 1) * lanes]
        out_ref[:, columns] = turned[tile].astype(jnp.bfloat16)


def owner_kernel(scale, order, slots, recv, query, out_ref, grads, per_example):
    blocks, height, width = recv.shape
    rank = grads.shape[1]
    rows = width
    half_rows = rows // 2
    examples = height - rank - half_rows
    pairs = rank // 2
    first_half = lax.broadcasted_iota(jnp.int32, (half_rows, width), 1) < rank

    def one(b):
        counts = recv[b, rank + half_rows :, :].astype(jnp.float32)
        slot = b % grads.shape[0]
        grads[slot] = recv[b, :rank, :].astype(jnp.float32)
        acts = recv[b, rank : rank + half_rows, :]
        swapped = jnp.concatenate([acts[:, rank:], acts[:, :rank]], axis=1)
        zero = jnp.zeros_like(acts)
        weights = jnp.concatenate(
            [
                jnp.where(first_half, acts, zero),
                jnp.where(first_half, swapped, zero),
                jnp.where(first_half, zero, swapped),
                jnp.where(first_half, zero, acts),
            ],
            axis=0,
        )
        columns = []
        for parity in range(2):
            pieces = [grads[slot, pl.ds(2 * p + parity, 1), :] * counts for p in range(pairs)]
            columns.append(jnp.concatenate(pieces, axis=0).astype(jnp.bfloat16))
        weighted = jnp.concatenate(columns, axis=1)
        return jnp.dot(weighted, weights, preferred_element_type=jnp.float32) * scale

    for b in range(0, blocks, 2):
        first, second = one(slots[b]), one(slots[b + 1])
        for p in range(pairs):
            piece = slice(p * examples, (p + 1) * examples)
            per_example[b * examples : (b + 2) * examples, p * width : (p + 1) * width] = jnp.concatenate(
                [first[piece], second[piece]], axis=0
            ).astype(jnp.bfloat16)

    scores = jnp.dot(per_example[...], query[...], preferred_element_type=jnp.float32).T
    tile = out_ref.shape[1]
    for slot, member in enumerate(order):
        out_ref[slot] = scores[member * tile : (member + 1) * tile]


def per_device(owners, act_table, grad_table, token_rows, left_inv, right_inv, query_grads):
    rows, columns = act_table.shape
    examples, tokens = token_rows.shape
    local_modules, rank, _ = left_inv.shape
    queries = query_grads.shape[0]
    width = 2 * rank
    lanes = min(queries, 128)
    assert queries % lanes == 0
    assert local_modules == 1 and columns == owners * rank and owners % 2 == 0
    assert rows == width and tokens <= 256 and examples % 8 == 0
    height = rank + rows // 2 + examples

    order = member_order(owners, owners * FIRST_OUT // 16)
    back = member_order(owners, owners * FIRST_BACK // 16)
    slots = [order.index(member) for member in range(owners)]

    def exchange(pieces, order):
        return lax.all_to_all(
            pieces, "module", split_axis=0, concat_axis=0, axis_index_groups=[order], tiled=True
        )

    packed = pl.pallas_call(
        functools.partial(pack_kernel, slots),
        out_shape=jax.ShapeDtypeStruct((owners, height, width), jnp.bfloat16),
        in_specs=[pl.BlockSpec(memory_space=pltpu.HBM)] * 3,
        out_specs=pl.BlockSpec(memory_space=pltpu.HBM),
        scratch_shapes=[
            pltpu.VMEM((rows, columns), jnp.bfloat16),
            pltpu.VMEM((rows, columns), jnp.bfloat16),
            pltpu.VMEM((examples, tokens), jnp.int32),
            pltpu.VMEM((owners, height, width), jnp.bfloat16),
            pltpu.SemaphoreType.DMA((3,)),
            pltpu.SemaphoreType.DMA((2,)),
        ],
        name="pack",
    )(act_table, grad_table, token_rows)
    recv = exchange(packed, order)

    prepared = pl.pallas_call(
        query_kernel,
        out_shape=jax.ShapeDtypeStruct((rank * rank, queries), jnp.bfloat16),
        scratch_shapes=[
            pltpu.VMEM((4 * rank, 4 * rank), jnp.bfloat16),
            pltpu.VMEM((queries // lanes, rank * rank, lanes), jnp.float32),
        ],
        cost_estimate=pl.CostEstimate(
            flops=4 * queries * rank**3, bytes_accessed=4 * queries * rank**2, transcendentals=0
        ),
        compiler_params=pltpu.CompilerParams(vmem_limit_bytes=VMEM_LIMIT),
        name="prepare",
    )(query_grads.reshape(queries, rank * rank), left_inv, right_inv)

    partial = pl.pallas_call(
        functools.partial(owner_kernel, 1.0 / math.sqrt(tokens), back, slots),
        out_shape=jax.ShapeDtypeStruct((owners, queries // owners, owners * examples), jnp.float32),
        scratch_shapes=[
            pltpu.VMEM((4, rank, rows), jnp.float32),
            pltpu.VMEM((owners * examples, rank * rank), jnp.bfloat16),
        ],
        compiler_params=pltpu.CompilerParams(vmem_limit_bytes=VMEM_LIMIT),
        name="owner",
    )(recv, prepared)

    return jnp.sum(exchange(partial, back), axis=0)


def solution(mesh):
    placed = (
        P(("groups", "module"), None),
        P(("groups", "module"), None),
        P(("groups", "module"), None),
        P("module", None, None),
        P("module", None, None),
        P("groups", "module", None),
    )
    return jax.shard_map(
        functools.partial(per_device, mesh.shape["module"]),
        mesh=mesh,
        in_specs=placed,
        out_specs=P(("groups", "module"), None),
        check_vma=False,
    )
```

```python
import functools
import math

import jax
import jax.numpy as jnp
from jax import lax
from jax.experimental import pallas as pl
from jax.experimental.pallas import tpu as pltpu
from jax.sharding import PartitionSpec as P


VMEM_LIMIT = 32 * 1024 * 1024
FIRST_OUT, FIRST_BACK = 9, 11
MOST_HOPPING = 16


def member_order(members, first):
    def hops(i):
        return abs((i >> 2) - (first >> 2)) + (((i ^ first) >> 1) & 1)

    return [first] + sorted((i for i in range(members) if i != first), key=lambda i: (-hops(i), i))


def pack_kernel(slots, act_hbm, grad_hbm, tok_hbm, out_hbm, act, grad, tok, packed, in_sem, out_sem):
    owners = out_hbm.shape[0]
    rows = act.shape[0]
    rank = act.shape[1] // owners
    half = rows // 2
    examples, tokens = tok.shape
    tok_copy = pltpu.make_async_copy(tok_hbm, tok, in_sem.at[0])
    grad_copy = pltpu.make_async_copy(grad_hbm, grad, in_sem.at[1])
    act_copy = pltpu.make_async_copy(act_hbm, act, in_sem.at[2])
    tok_copy.start()
    grad_copy.start()
    act_copy.start()

    tok_copy.wait()
    local = tok[...]
    row_of_lane = lax.broadcasted_iota(jnp.int32, (examples, rows), 1)
    counts = jnp.zeros((examples, rows), jnp.float32)
    for t in range(tokens):
        counts += jnp.where(local[:, t : t + 1] == row_of_lane, 1.0, 0.0)
    counts = counts.astype(jnp.bfloat16)

    grad_copy.wait()
    act_copy.wait()
    departures = []
    ready = set()
    share = owners // out_sem.shape[0]
    for slot in range(owners):
        pair = slots.index(slot) // 2
        if pair not in ready:
            ready.add(pair)
            wide = slice(2 * pair * rank, 2 * (pair + 1) * rank)
            turned = act[:, wide].T
            plain = grad[:, wide]
            for side in range(2):
                columns = slice(side * rank, (side + 1) * rank)
                to = slots[2 * pair + side]
                packed[to, :rank, :] = turned[columns, :]
                packed[to, rank : rank + half, :] = jnp.concatenate([plain[:half, columns], plain[half:, columns]], axis=1)
                packed[to, rank + half :, :] = counts
        if (slot + 1) % share == 0:
            block = pl.ds(slot + 1 - share, share)
            departures.append(pltpu.make_async_copy(packed.at[block], out_hbm.at[block], out_sem.at[slot // share]))
            departures[-1].start()
    for copy in departures:
        copy.wait()


def query_kernel(query_ref, left_ref, right_ref, out_ref, turned):
    rank = left_ref.shape[-1]
    tiles, _, lanes = turned.shape
    some = 4
    step = some * rank
    groups = rank // some

    def iota(shape, dim):
        return lax.broadcasted_iota(jnp.int32, shape, dim)

    repeat = jnp.where(iota((step, rank), 0) // some == iota((step, rank), 1), 1.0, 0.0).astype(jnp.bfloat16)
    right = jnp.concatenate([right_ref[0]] * some, axis=1)
    spread = jnp.dot(repeat, right, preferred_element_type=jnp.float32)
    spread = jnp.where(iota((step, step), 0) % some == iota((step, step), 1) // rank, spread, 0.0).astype(jnp.bfloat16)
    wide = 2 * rank
    column = iota((rank, wide), 1)
    chosen = jnp.where(iota((rank, wide), 0) == some * (column // (2 * some)) + column % some, 1.0, 0.0)
    left = left_ref[0].astype(jnp.float32).T.astype(jnp.bfloat16)
    mixed = jnp.dot(left, chosen.astype(jnp.bfloat16), preferred_element_type=jnp.float32)
    second = column // some % 2 == 1
    mixed = jnp.concatenate([jnp.where(second, 0.0, mixed), jnp.where(second, mixed, 0.0)], axis=0).astype(jnp.bfloat16)
    mixed = jnp.concatenate([mixed, mixed], axis=1)
    for tile in range(tiles):
        columns = slice(tile * lanes, (tile + 1) * lanes)
        for t in range(groups):
            turned[tile, t * step : (t + 1) * step, :] = lax.dot_general(
                spread,
                query_ref[columns, t * step : (t + 1) * step],
                (((1,), (1,)), ((), ())),
                preferred_element_type=jnp.float32,
            )
        for pair in range(rank // 2):
            at = pair * 2 * some
            value = jnp.concatenate(
                [turned[tile, t * step + at : t * step + at + 2 * some, :] for t in range(groups)], axis=0
            )
            high = value.astype(jnp.bfloat16)
            low = (value - high.astype(jnp.float32)).astype(jnp.bfloat16)
            product = jnp.dot(mixed, jnp.concatenate([high, low], axis=0), preferred_element_type=jnp.float32)
            out_ref[pair * wide : (pair + 1) * wide, columns] = product.astype(jnp.bfloat16)


def owner_kernel(scale, order, slots, recv, query, out_ref, grads, per_example):
    blocks, height, width = recv.shape
    rank = grads.shape[1]
    rows = width
    half_rows = rows // 2
    examples = height - rank - half_rows
    pairs = rank // 2
    first_half = lax.broadcasted_iota(jnp.int32, (half_rows, width), 1) < rank

    def one(b):
        counts = recv[b, rank + half_rows :, :].astype(jnp.float32)
        slot = b % grads.shape[0]
        grads[slot] = recv[b, :rank, :].astype(jnp.float32)
        acts = recv[b, rank : rank + half_rows, :]
        swapped = jnp.concatenate([acts[:, rank:], acts[:, :rank]], axis=1)
        zero = jnp.zeros_like(acts)
        weights = jnp.concatenate(
            [
                jnp.where(first_half, acts, zero),
                jnp.where(first_half, swapped, zero),
                jnp.where(first_half, zero, swapped),
                jnp.where(first_half, zero, acts),
            ],
            axis=0,
        )
        columns = []
        for parity in range(2):
            pieces = [grads[slot, pl.ds(2 * p + parity, 1), :] * counts for p in range(pairs)]
            columns.append(jnp.concatenate(pieces, axis=0).astype(jnp.bfloat16))
        weighted = jnp.concatenate(columns, axis=1)
        return jnp.dot(weighted, weights, preferred_element_type=jnp.float32) * scale

    for b in range(0, blocks, 2):
        first, second = one(slots[b]), one(slots[b + 1])
        for p in range(pairs):
            piece = slice(p * examples, (p + 1) * examples)
            per_example[b * examples : (b + 2) * examples, p * width : (p + 1) * width] = jnp.concatenate(
                [first[piece], second[piece]], axis=0
            ).astype(jnp.bfloat16)

    scores = jnp.dot(per_example[...], query[...], preferred_element_type=jnp.float32).T
    tile = out_ref.shape[1]
    for slot, member in enumerate(order):
        out_ref[slot] = scores[member * tile : (member + 1) * tile]


def hop_order(chips):
    far = sorted(range(chips // 2, chips), key=lambda k: (k & 1, -k))
    near = list(range(1, chips // 2))
    order = []
    for at, k in enumerate(far):
        order.append(k)
        order.extend(near[at : at + 1])
    return order


def hop_pack_kernel(act_hbm, grad_hbm, tok_hbm, *refs):
    chips = len(refs) - 6
    outs = refs[:chips]
    act, grad, tok, packed, in_sem, out_sem = refs[chips:]
    chip = lax.axis_index("module") // 2
    rows = act.shape[0]
    rank = act.shape[1] // (2 * chips)
    half = rows // 2
    examples, tokens = tok.shape
    tok_copy = pltpu.make_async_copy(tok_hbm, tok, in_sem.at[0])
    grad_copy = pltpu.make_async_copy(grad_hbm, grad, in_sem.at[1])
    act_copy = pltpu.make_async_copy(act_hbm, act, in_sem.at[2])
    tok_copy.start()
    grad_copy.start()
    act_copy.start()

    tok_copy.wait()
    local = tok[...]
    row_of_lane = lax.broadcasted_iota(jnp.int32, (examples, rows), 1)
    counts = jnp.zeros((examples, rows), jnp.float32)
    for t in range(tokens):
        counts += jnp.where(local[:, t : t + 1] == row_of_lane, 1.0, 0.0)
    counts = counts.astype(jnp.bfloat16)

    grad_copy.wait()
    act_copy.wait()
    for other in range(chips):
        wide = slice(2 * other * rank, 2 * (other + 1) * rank)
        turned = act[:, wide].T
        plain = grad[:, wide]
        distance = chip ^ other
        for side in range(2):
            columns = slice(side * rank, (side + 1) * rank)
            packed[distance, side, :rank, :] = turned[columns, :]
            packed[distance, side, rank : rank + half, :] = jnp.concatenate(
                [plain[:half, columns], plain[half:, columns]], axis=1
            )
            packed[distance, side, rank + half :, :] = counts
    departures = [pltpu.make_async_copy(packed.at[k], outs[k], out_sem.at[k]) for k in range(chips)]
    for copy in departures:
        copy.start()
    for copy in departures:
        copy.wait()


def hop_owner_kernel(scale, order, *refs):
    chips = len(refs) - 6
    arrived = refs[:chips]
    own_query, other_query, out_ref, grads, per_example, placed = refs[chips:]
    core = lax.axis_index("module") % 2
    chip = lax.axis_index("module") // 2
    _, height, width = arrived[0].shape
    rank = grads.shape[1]
    half_rows = width // 2
    examples = height - rank - half_rows
    pairs = rank // 2
    first_half = lax.broadcasted_iota(jnp.int32, (half_rows, width), 1) < rank

    def one(block, side, slot):
        counts = block[side, rank + half_rows :, :].astype(jnp.float32)
        grads[slot] = block[side, :rank, :].astype(jnp.float32)
        acts = block[side, rank : rank + half_rows, :]
        swapped = jnp.concatenate([acts[:, rank:], acts[:, :rank]], axis=1)
        zero = jnp.zeros_like(acts)
        weights = jnp.concatenate(
            [
                jnp.where(first_half, acts, zero),
                jnp.where(first_half, swapped, zero),
                jnp.where(first_half, zero, swapped),
                jnp.where(first_half, zero, acts),
            ],
            axis=0,
        )
        columns = []
        for parity in range(2):
            pieces = [grads[slot, pl.ds(2 * p + parity, 1), :] * counts for p in range(pairs)]
            columns.append(jnp.concatenate(pieces, axis=0).astype(jnp.bfloat16))
        weighted = jnp.concatenate(columns, axis=1)
        return jnp.dot(weighted, weights, preferred_element_type=jnp.float32) * scale

    scores = []
    for turn, query in enumerate((own_query, other_query)):
        side = core if turn == 0 else 1 - core
        for k in range(0, chips, 2):
            slot = (turn * chips + k) % grads.shape[0]
            first, second = one(arrived[k], side, slot), one(arrived[k + 1], side, slot + 1)
            for p in range(pairs):
                piece = slice(p * examples, (p + 1) * examples)
                per_example[turn, k * examples : (k + 2) * examples, p * width : (p + 1) * width] = jnp.concatenate(
                    [first[piece], second[piece]], axis=0
                ).astype(jnp.bfloat16)
        scores.append(jnp.dot(per_example[turn], query[...], preferred_element_type=jnp.float32))
    total = scores[0] + scores[1]
    placed[...] = jnp.zeros_like(placed)
    for k in range(chips):
        block = 2 * (chip ^ k) + core
        placed[pl.ds(pl.multiple_of(block * examples, examples), examples), :] = total[k * examples : (k + 1) * examples]
    turned = placed[...].T
    tile = out_ref.shape[1]
    for slot, member in enumerate(order):
        out_ref[slot] = turned[member * tile : (member + 1) * tile]


def per_device(owners, act_table, grad_table, token_rows, left_inv, right_inv, query_grads):
    rows, columns = act_table.shape
    examples, tokens = token_rows.shape
    local_modules, rank, _ = left_inv.shape
    queries = query_grads.shape[0]
    width = 2 * rank
    lanes = min(queries, 128)
    assert queries % lanes == 0
    assert local_modules == 1 and columns == owners * rank and owners % 4 == 0
    assert rows == width and tokens <= 256 and examples % 8 == 0
    height = rank + rows // 2 + examples
    chips = owners // 2
    scale = 1.0 / math.sqrt(tokens)
    back = member_order(owners, owners * FIRST_BACK // 16)
    limit = pltpu.CompilerParams(vmem_limit_bytes=VMEM_LIMIT)
    partial_shape = jax.ShapeDtypeStruct((owners, queries // owners, owners * examples), jnp.float32)
    tables = [
        pltpu.VMEM((rows, columns), jnp.bfloat16),
        pltpu.VMEM((rows, columns), jnp.bfloat16),
        pltpu.VMEM((examples, tokens), jnp.int32),
    ]

    def exchange(pieces, order):
        return lax.all_to_all(
            pieces, "module", split_axis=0, concat_axis=0, axis_index_groups=[order], tiled=True
        )

    def prepare():
        return pl.pallas_call(
            query_kernel,
            out_shape=jax.ShapeDtypeStruct((rank * rank, queries), jnp.bfloat16),
            scratch_shapes=[
                pltpu.VMEM((queries // lanes, rank * rank, lanes), jnp.float32),
            ],
            cost_estimate=pl.CostEstimate(
                flops=4 * queries * rank**3, bytes_accessed=4 * queries * rank**2, transcendentals=0
            ),
            compiler_params=limit,
            name="prepare",
        )(query_grads.reshape(queries, rank * rank), left_inv, right_inv)

    def by_exchange():
        order = member_order(owners, owners * FIRST_OUT // 16)
        slots = [order.index(member) for member in range(owners)]
        packed = pl.pallas_call(
            functools.partial(pack_kernel, slots),
            out_shape=jax.ShapeDtypeStruct((owners, height, width), jnp.bfloat16),
            in_specs=[pl.BlockSpec(memory_space=pltpu.HBM)] * 3,
            out_specs=pl.BlockSpec(memory_space=pltpu.HBM),
            scratch_shapes=tables
            + [
                pltpu.VMEM((owners, height, width), jnp.bfloat16),
                pltpu.SemaphoreType.DMA((3,)),
                pltpu.SemaphoreType.DMA((2,)),
            ],
            name="pack",
        )(act_table, grad_table, token_rows)
        recv = exchange(packed, order)
        return pl.pallas_call(
            functools.partial(owner_kernel, scale, back, slots),
            out_shape=partial_shape,
            scratch_shapes=[
                pltpu.VMEM((4, rank, rows), jnp.float32),
                pltpu.VMEM((owners * examples, rank * rank), jnp.bfloat16),
            ],
            compiler_params=limit,
            name="owner",
        )(recv, prepare())

    def by_hops():
        packed = pl.pallas_call(
            hop_pack_kernel,
            out_shape=[jax.ShapeDtypeStruct((2, height, width), jnp.bfloat16)] * chips,
            in_specs=[pl.BlockSpec(memory_space=pltpu.HBM)] * 3,
            out_specs=[pl.BlockSpec(memory_space=pltpu.HBM)] * chips,
            scratch_shapes=tables
            + [
                pltpu.VMEM((chips, 2, height, width), jnp.bfloat16),
                pltpu.SemaphoreType.DMA((3,)),
                pltpu.SemaphoreType.DMA((chips,)),
            ],
            name="pack",
        )(act_table, grad_table, token_rows)
        arrived = list(packed)
        for k in hop_order(chips):
            arrived[k] = lax.ppermute(packed[k], "module", [(i, i ^ (2 * k)) for i in range(owners)])
        prepared = prepare()
        swapped = lax.ppermute(prepared, "module", [(i, i ^ 1) for i in range(owners)])
        return pl.pallas_call(
            functools.partial(hop_owner_kernel, scale, back),
            out_shape=partial_shape,
            scratch_shapes=[
                pltpu.VMEM((4, rank, rows), jnp.float32),
                pltpu.VMEM((2, chips * examples, rank * rank), jnp.bfloat16),
                pltpu.VMEM((owners * examples, queries), jnp.float32),
            ],
            compiler_params=limit,
            name="owner",
        )(*arrived, prepared, swapped)

    partial = by_hops() if hopping(owners) else by_exchange()
    return jnp.sum(exchange(partial, back), axis=0)


def hopping(owners):
    return owners & (owners - 1) == 0 and owners <= MOST_HOPPING


def solution(mesh):
    placed = (
        P(("groups", "module"), None),
        P(("groups", "module"), None),
        P(("groups", "module"), None),
        P("module", None, None),
        P("module", None, None),
        P("groups", "module", None),
    )
    owners = mesh.shape["module"]
    return jax.shard_map(
        functools.partial(per_device, owners),
        mesh=mesh,
        in_specs=placed,
        out_specs=P(("groups", "module"), None),
        check_vma=False,
    )
```
